128 devices in a mesh: ctx: 16 (over y_hi, x, core), tp: 8 (over y_lo, z).
Axes of the slice: x: 4, y: 4 (y_hi: 2, y_lo: 2; y = y_hi * 2 + y_lo), z: 4, core: 2. Of those that a mesh axis runs over, the one named last changes fastest.
Arguments:
- tokens: bfloat16 [2048, 4096], P('ctx', 'tp'), may hold values from -6 to 6
- in_weight: bfloat16 [4096, 3, 4096], P(None, None, 'tp'), may hold values from -0.09375 to 0.09375
- conv_weight: float32 [7, 3, 4096], P(None, None, 'tp'), may hold values from -2 to 2
- filters: bfloat16 [2048, 4096], P(None, 'tp'), may hold values from -1 to 1
- skip_gain: float32 [4096], P('tp'), may hold values from -4 to 4
Outputs:
- mixed_out: bfloat16 [2048, 4096], P('ctx', 'tp')
The draws below stay inside these ranges and needn't reach their ends.
All inputs are finite; a program needn't handle non-finite values.
Results may differ from the reference program's by a relative error of at most 0.0095.
Values may be sent and summed in bfloat16 or wider, within the bound.
A program may use at most 128 MiB of HBM per device.

```python
import jax
import jax.numpy as jnp

D = 4096
TAPS = 7
L = 2048
CH = 4096


def draw_filters(key, part):
    first_key, second_key = jax.random.split(key)
    positions = jnp.arange(L, dtype=jnp.float32)[:, None]
    lifetime = jnp.exp(jax.random.uniform(first_key, (CH,), jnp.float32, jnp.log(20.0), jnp.log(4.0 * L)))
    roughness = jnp.clip(jax.random.normal(second_key, (L, CH), jnp.float32), -4.0, 4.0)
    return (roughness * jnp.exp(-positions / lifetime[None, :]) / jnp.sqrt(lifetime)[None, :]).astype(jnp.bfloat16)


def block_scale(stream_key, extent, pieces, least, high):
    def one(position, parts):
        steps = jax.random.uniform(jax.random.fold_in(jax.random.fold_in(stream_key, 6), position), (parts,), jnp.float32, least / len(pieces), high / len(pieces))
        return jnp.repeat(jnp.exp(steps), extent[position] // parts).reshape((-1,) + (1,) * (len(extent) - position - 1))

    level = one(*pieces[0])
    for cut in pieces[1:]:
        level = level * one(*cut)
    return level


def normal_values(stream_key, extent, scale, most, pieces=(), held_as=jnp.bfloat16):
    drawn = jax.random.normal(stream_key, extent, jnp.float32) * scale
    if len(pieces) > 0:
        drawn = block_scale(stream_key, extent, pieces, -0.22, 0.18) * drawn
    return jnp.clip(drawn, min=-most, max=most).astype(held_as)


def setup_inputs(seed: int = 0) -> dict:
    streams_of = jax.random.split(jax.random.key(seed), 6)
    tokens = normal_values(streams_of[0], (L, D), 1.0, 6.0, ((0, 16), (1, 8)))
    in_weight = normal_values(streams_of[1], (D, 3, CH), D ** -0.5, 0.09375, ((2, 8),))
    conv_weight = normal_values(streams_of[2], (TAPS, 3, CH), TAPS ** -0.5, 2.0, ((2, 8),), jnp.float32)
    filters = draw_filters(jax.random.fold_in(streams_of[5], 71), 0)
    skip_gain = normal_values(streams_of[4], (CH,), 1.0, 4.0, ((0, 8),), jnp.float32)
    return dict(tokens=tokens, in_weight=in_weight, conv_weight=conv_weight, filters=filters, skip_gain=skip_gain)


def reference(tokens, in_weight, conv_weight, filters, skip_gain):
    length = tokens.shape[0]
    flat_weight = in_weight.reshape(D, 3 * CH)
    projected = jnp.dot(tokens, flat_weight, preferred_element_type=jnp.float32).astype(jnp.bfloat16)
    projected = projected.reshape(length, 3, CH).astype(jnp.float32)
    extended = jnp.concatenate([jnp.zeros((TAPS - 1, 3, CH), jnp.float32), projected], 0)
    branches = conv_weight[0] * extended[0:length]
    for tap_index in range(1, TAPS):
        branches = branches + conv_weight[tap_index] * extended[tap_index:tap_index + length]
    gate_branch = branches[:, 0]
    product = (branches[:, 1] * branches[:, 2]).astype(jnp.bfloat16)
    product_wide = product.astype(jnp.float32)
    dft_length = 2 * length
    spectra = jnp.fft.rfft(filters.astype(jnp.float32), n=dft_length, axis=0) * jnp.fft.rfft(product_wide, n=dft_length, axis=0)
    convolved = jnp.fft.irfft(spectra, n=dft_length, axis=0)[:length]
    return (gate_branch * (convolved + skip_gain * product_wide)).astype(jnp.bfloat16)
```

```python
import functools

import jax
import jax.numpy as jnp
import ml_dtypes
import numpy as np
from jax import lax
from jax.experimental import pallas as pl
from jax.experimental.pallas import tpu as pltpu
from jax.sharding import PartitionSpec as P

TAPS = 7
MESH = pl.DeviceIdType.MESH
ROWS = 128
HALO = 8
PAD = 16
DEPTH = 512
CH = 512
NCTX = 16
NZ = 4
PART = CH // NCTX
SUB = 32
F32 = jnp.float32
BF16 = jnp.bfloat16


def split(table):
    high = table.astype(ml_dtypes.bfloat16)
    low = (table - high.astype(np.float64)).astype(ml_dtypes.bfloat16)
    return high, low


def tables():
    size = 2 * ROWS
    time = np.arange(ROWS)[:, None]
    freq = np.arange(ROWS)[None, :]
    angle = 2 * np.pi * (time * freq % size) / size
    imag = -np.sin(angle)
    imag[:, 0] = np.where(np.arange(ROWS) % 2 == 0, 1.0, -1.0)
    forward = np.concatenate([np.cos(angle), imag], 1)
    weight = np.where(np.arange(ROWS) == 0, 1.0, 2.0)[None, :] / size
    back_real = np.cos(angle) * weight
    back_imag = -np.sin(angle) * weight
    back_imag[:, 0] = np.where(np.arange(ROWS) % 2 == 0, 1.0, -1.0) / size
    inverse = np.concatenate([back_real, back_imag], 1).T
    return (*split(forward), *split(inverse))


def nt_dot(left, right):
    return lax.dot_general(left, right, (((1,), (1,)), ((), ())), preferred_element_type=F32)


def dot(left, right):
    return jnp.dot(left, right, preferred_element_type=F32)


def eye(rows, columns, offset):
    row = lax.broadcasted_iota(jnp.int32, (rows, columns), 0)
    column = lax.broadcasted_iota(jnp.int32, (rows, columns), 1)
    return row + offset == column


def kernel(
    tokens, weight, taps, filters, skip, fwd_hi, fwd_lo, inv_hi, inv_lo, out,
    slots, w_v, taps_v, filt_v, skip_v, fh_v, fl_v, ih_v, il_v,
    total, ext, gate, filt_t, spec, gain_re, gain_im, gain_ny, psend, precv, yhat, ysend, yrecv,
    w_sem, load_sem, own_sem, g_send, g_recv, h_send, h_recv, p_send, p_recv, y_send, y_recv,
):
    ctx = lax.axis_index("ctx")
    tp = lax.axis_index("tp")
    y, z = tp // NZ, tp % NZ
    y_side = (1 - y) * NZ + z
    z_up = y * NZ + (z + 1) % NZ
    z_down = y * NZ + (z + NZ - 1) % NZ

    def peer(mask):
        other = ctx
        for bit in (1, 2, 4, 8):
            if mask & bit:
                other = other + bit * (1 - 2 * ((ctx // bit) % 2))
        return other

    for index in range(2 * NZ):
        slots[index, pl.ds(0, PAD)] = jnp.zeros((PAD, DEPTH), BF16)

    barrier = pltpu.get_barrier_semaphore()
    for side in (y_side, z_up, z_down):
        pl.semaphore_signal(barrier, inc=1, device_id={"ctx": ctx, "tp": side}, device_id_type=MESH)
    for mask in range(1, NCTX):
        pl.semaphore_signal(barrier, inc=1, device_id={"ctx": peer(mask), "tp": tp}, device_id_type=MESH)

    loads = [
        pltpu.make_async_copy(src, dst, load_sem.at[index])
        for index, (src, dst) in enumerate(
            [
                (filters.at[:, pl.ds(pl.multiple_of(ctx // 4 * 128, 128), 128)], filt_v),
                (fwd_hi, fh_v),
                (fwd_lo, fl_v),
                (inv_hi, ih_v),
                (inv_lo, il_v),
                (taps, taps_v),
                (skip, skip_v),
            ]
        )
    ]
    own = pltpu.make_async_copy(tokens, slots.at[0, pl.ds(PAD, ROWS)], own_sem.at[0])
    own.start()
    for load in loads:
        load.start()

    def source(dy, dz):
        there = (1 - y) if dy else y
        return there * NZ + (z + dz) % NZ

    def weight_load(dy, dz):
        rows = pl.ds(pl.multiple_of(source(dy, dz) * DEPTH, DEPTH), DEPTH)
        return pltpu.make_async_copy(weight.at[:, rows], w_v.at[:, rows], w_sem.at[dy * NZ + dz])

    order = [(0, 0), (1, 0), (0, 3), (0, 1), (0, 2), (1, 3), (1, 1), (1, 2)]
    for dy, dz in order:
        weight_load(dy, dz).start()

    pl.semaphore_wait(barrier, 3 + NCTX - 1)

    def rows_of(piece):
        return pl.ds(PAD + piece * SUB, SUB)

    pieces = ROWS // SUB
    low = list(range(pieces // 2))
    high = list(range(pieces // 2, pieces))

    def gather_copy(src_slot, piece, dst_slot, side):
        first = src_slot == (0, 0)
        src = tokens.at[pl.ds(piece * SUB, SUB)] if first else slots.at[src_slot[0] * NZ + src_slot[1], rows_of(piece)]
        index = dst_slot[0] * NZ + dst_slot[1]
        return pltpu.make_async_remote_copy(
            src_ref=src,
            dst_ref=slots.at[index, rows_of(piece)],
            send_sem=g_send.at[index, piece],
            recv_sem=g_recv.at[index, piece],
            device_id={"ctx": ctx, "tp": side},
            device_id_type=MESH,
        )

    sent = []

    def send(src_slot, piece, dst_slot, side):
        copy = gather_copy(src_slot, piece, dst_slot, side)
        copy.start()
        sent.append(copy)

    def arrived(slot, piece):
        gather_copy((1, 1), piece, slot, z_up).wait_recv()

    halo_rows = pl.ds(PAD - HALO, HALO)

    def halo_copy(src_slot, dst_slot, device):
        index = dst_slot[0] * NZ + dst_slot[1]
        src = slots.at[src_slot[0] * NZ + src_slot[1], halo_rows]
        if dst_slot == (0, 0):
            src = tokens.at[pl.ds(ROWS - HALO, HALO)]
        return pltpu.make_async_remote_copy(
            src_ref=src,
            dst_ref=slots.at[index, halo_rows],
            send_sem=h_send.at[index],
            recv_sem=h_recv.at[index],
            device_id=device,
            device_id_type=MESH,
        )

    @pl.when(ctx < NCTX - 1)
    def _():
        halo_copy((0, 0), (0, 0), {"ctx": ctx + 1, "tp": tp}).start()

    for a, b in zip(high, low):
        send((0, 0), a, (1, 0), y_side)
        send((0, 0), a, (0, 3), z_up)
        send((0, 0), b, (0, 1), z_down)
        send((0, 0), b, (1, 0), y_side)
    for a, b in zip(high, low):
        send((0, 0), b, (0, 3), z_up)
        send((0, 0), a, (0, 1), z_down)

    halo_hops = [
        ((0, 0), (1, 0), y_side),
        ((0, 0), (0, 3), z_up),
        ((0, 0), (0, 1), z_down),
        ((0, 3), (0, 2), z_up),
        ((1, 0), (1, 3), z_up),
        ((1, 0), (1, 1), z_down),
        ((1, 3), (1, 2), z_up),
    ]

    def halo_arrived(slot):
        halo_copy((0, 1), slot, {"ctx": ctx, "tp": z_up}).wait_recv()

    def halo_from(slot):
        for src, dst, side in halo_hops:
            if src == slot:
                halo_copy(src, dst, {"ctx": ctx, "tp": side}).start()

    def halo_step(slot):
        @pl.when(ctx > 0)
        def _():
            halo_arrived(slot)
            halo_from(slot)

    for load in loads:
        load.wait()
    pick = eye(PART, 128, ctx % 4 * PART)
    across = nt_dot(pick.astype(BF16), filt_v[...]).astype(BF16)
    for block in range(NCTX):
        filt_t[pl.ds(block * PART, PART)] = across[:, block * ROWS : (block + 1) * ROWS]
    spec[...] = dot(filt_t[...], fh_v[...]) + dot(filt_t[...], fl_v[...])
    lane = lax.broadcasted_iota(jnp.int32, (PART, ROWS), 1)
    swap = jnp.where(lane % 2 == 0, 1.0, -1.0).astype(F32)
    first_lane = lane == 0
    for block in range(NCTX):
        now = pl.ds(block * PART, PART)
        real = spec[now, :ROWS]
        imag = spec[now, ROWS:]
        if block:
            before = pl.ds((block - 1) * PART, PART)
            real = real + swap * spec[before, :ROWS]
            imag = imag + swap * spec[before, ROWS:]
        gain_re[now] = real
        gain_im[now] = jnp.where(first_lane, 0.0, imag)
        gain_ny[now] = jnp.where(first_lane, imag, real)

    own.wait()
    halo_step((0, 0))

    def project(slot, start):
        weight_load(*slot).wait()
        index = slot[0] * NZ + slot[1]
        rows = pl.ds(pl.multiple_of(source(*slot) * DEPTH, DEPTH), DEPTH)

        def branch(b, carry):
            term = dot(slots[index], w_v[b, rows])
            total[b] = term if start else total[b] + term
            return carry

        lax.fori_loop(0, 3, branch, 0)

    project((0, 0), True)

    for a, b in zip(high, low):
        arrived((1, 0), a)
        send((1, 0), a, (1, 3), z_up)
        arrived((0, 1), b)
        send((0, 1), b, (0, 2), z_down)
        arrived((0, 3), a)
        send((0, 3), a, (0, 2), z_up)
        arrived((1, 0), b)
        send((1, 0), b, (1, 1), z_down)
    halo_step((1, 0))
    project((1, 0), False)
    for a, b in zip(high, low):
        arrived((0, 3), b)
        send((0, 3), b, (1, 3), y_side)
        arrived((0, 1), a)
        send((0, 1), a, (1, 1), y_side)
    halo_step((0, 3))
    halo_step((0, 1))
    project((0, 3), False)
    for a, b in zip(high, low):
        arrived((1, 3), a)
        send((1, 3), a, (1, 2), z_up)
        arrived((1, 1), b)
        send((1, 1), b, (1, 2), z_down)
    halo_step((1, 3))
    project((0, 1), False)
    for piece in range(pieces):
        arrived((0, 2), piece)
    halo_step((0, 2))
    project((0, 2), False)
    for piece in low:
        arrived((1, 3), piece)
    project((1, 3), False)
    for piece in high:
        arrived((1, 1), piece)
    halo_step((1, 1))
    project((1, 1), False)
    for piece in range(pieces):
        arrived((1, 2), piece)
    halo_step((1, 2))
    project((1, 2), False)

    ident = eye(ROWS, ROWS, 0).astype(BF16)
    for group in range(CH // 128):
        lanes = slice(group * 128, (group + 1) * 128)
        branches = []
        for b in range(3):
            ext[b] = total[b, :, lanes].astype(BF16).astype(F32)
            acc = taps_v[b, 0:1, lanes] * ext[b, pl.ds(PAD - TAPS + 1, ROWS)]
            for t in range(1, TAPS):
                acc = acc + taps_v[b, t : t + 1, lanes] * ext[b, pl.ds(PAD - TAPS + 1 + t, ROWS)]
            branches.append(acc)
        gate[:, lanes] = branches[0]
        product = (branches[1] * branches[2]).astype(BF16)
        turned = nt_dot(ident, product).astype(BF16)
        for part in range(128 // PART):
            psend[group * (128 // PART) + part] = turned[part * PART : (part + 1) * PART]

    far_first = [12, 13, 10, 11, 14, 15, 8, 9, 4, 5, 2, 3, 6, 7, 1]

    def exchange(send_buffer, recv_buffer, send_sem, recv_sem):
        copies = []
        for mask in far_first:
            other = peer(mask)
            copy = pltpu.make_async_remote_copy(
                src_ref=send_buffer.at[other],
                dst_ref=recv_buffer.at[ctx],
                send_sem=send_sem.at[mask],
                recv_sem=recv_sem.at[mask],
                device_id={"ctx": other, "tp": tp},
                device_id_type=MESH,
            )
            copy.start()
            copies.append(copy)
        recv_buffer[pl.ds(ctx, 1)] = send_buffer[pl.ds(ctx, 1)]
        for copy in copies:
            copy.wait()

    exchange(psend, precv, p_send, p_recv)

    block_rows = precv[...].reshape(NCTX * PART, ROWS)
    spec[...] = dot(block_rows, fh_v[...]) + dot(block_rows, fl_v[...])
    for block in range(NCTX):
        real = jnp.zeros((PART, ROWS), F32)
        imag = jnp.zeros((PART, ROWS), F32)
        for earlier in range(block + 1):
            lag = pl.ds((block - earlier) * PART, PART)
            src = pl.ds(earlier * PART, PART)
            p_real = spec[src, :ROWS]
            p_imag = spec[src, ROWS:]
            cross = gain_im[lag]
            real = real + gain_re[lag] * p_real - cross * p_imag
            imag = imag + gain_ny[lag] * p_imag + cross * p_real
        now = pl.ds(block * PART, PART)
        yhat[now, :ROWS] = real
        yhat[now, ROWS:] = imag
    both = yhat[...]
    upper = both.astype(BF16)
    lower = (both - upper.astype(F32)).astype(BF16)
    convolved = dot(upper, ih_v[...]) + dot(upper, il_v[...]) + dot(lower, ih_v[...])
    skip_row = skip_v[:, pl.ds(pl.multiple_of(ctx // 4 * 128, 128), 128)]
    skip_column = jnp.sum(jnp.where(pick, skip_row, 0.0), axis=1, keepdims=True)
    direct = skip_column[None] * precv[...].astype(F32)
    ysend[...] = (convolved.reshape(NCTX, PART, ROWS) + direct).astype(BF16)

    exchange(ysend, yrecv, y_send, y_recv)

    mixed = nt_dot(ident, yrecv[...].reshape(CH, ROWS))
    out[...] = (gate[...] * mixed).astype(BF16)

    for copy in sent:
        copy.wait_send()

    @pl.when(ctx < NCTX - 1)
    def _():
        halo_copy((0, 0), (0, 0), {"ctx": ctx + 1, "tp": tp}).wait_send()

    @pl.when(ctx > 0)
    def _():
        for src, dst, side in halo_hops:
            halo_copy(src, dst, {"ctx": ctx, "tp": side}).wait_send()


def local(tokens, in_weight, conv_weight, filters, skip_gain):
    any_space = pl.BlockSpec(memory_space=pl.ANY)
    dma = pltpu.SemaphoreType.DMA
    pieces = ROWS // SUB
    size = 2 * ROWS
    scratch = [
        pltpu.VMEM((2 * NZ, PAD + ROWS, DEPTH), BF16),
        pltpu.VMEM((3, 2 * NZ * DEPTH, CH), BF16),
        pltpu.VMEM((3, TAPS, CH), F32),
        pltpu.VMEM((NCTX * ROWS, 128), BF16),
        pltpu.VMEM((1, CH), F32),
        pltpu.VMEM((ROWS, size), BF16),
        pltpu.VMEM((ROWS, size), BF16),
        pltpu.VMEM((size, ROWS), BF16),
        pltpu.VMEM((size, ROWS), BF16),
        pltpu.VMEM((3, PAD + ROWS, CH), F32),
        pltpu.VMEM((3, PAD + ROWS, 128), F32),
        pltpu.VMEM((ROWS, CH), F32),
        pltpu.VMEM((NCTX * PART, ROWS), BF16),
        pltpu.VMEM((NCTX * PART, size), F32),
        pltpu.VMEM((NCTX * PART, ROWS), F32),
        pltpu.VMEM((NCTX * PART, ROWS), F32),
        pltpu.VMEM((NCTX * PART, ROWS), F32),
        pltpu.VMEM((NCTX, PART, ROWS), BF16),
        pltpu.VMEM((NCTX, PART, ROWS), BF16),
        pltpu.VMEM((NCTX * PART, size), F32),
        pltpu.VMEM((NCTX, PART, ROWS), BF16),
        pltpu.VMEM((NCTX, PART, ROWS), BF16),
        dma((2 * NZ,)),
        dma((7,)),
        dma((1,)),
        dma((2 * NZ, pieces)),
        dma((2 * NZ, pieces)),
        dma((2 * NZ,)),
        dma((2 * NZ,)),
        dma((NCTX,)),
        dma((NCTX,)),
        dma((NCTX,)),
        dma((NCTX,)),
    ]
    return pl.pallas_call(
        kernel,
        out_shape=jax.ShapeDtypeStruct((ROWS, CH), BF16),
        in_specs=[any_space] * 9,
        out_specs=pl.BlockSpec(memory_space=pltpu.VMEM),
        scratch_shapes=scratch,
        compiler_params=pltpu.CompilerParams(
            collective_id=0, has_side_effects=True, vmem_limit_bytes=56 * 1024 * 1024
        ),
        name="hyena",
    )(
        tokens,
        jnp.transpose(in_weight, (1, 0, 2)),
        jnp.transpose(conv_weight, (1, 0, 2)),
        filters,
        skip_gain.reshape(1, CH),
        *(jnp.asarray(table) for table in tables()),
    )


def solution(mesh):
    placed = (P("ctx", "tp"), P(None, None, "tp"), P(None, None, "tp"), P(None, "tp"), P("tp"))
    return jax.shard_map(local, mesh=mesh, in_specs=placed, out_specs=P("ctx", "tp"), check_vma=False)
```

```python
import functools

import jax
import jax.numpy as jnp
import ml_dtypes
import numpy as np
from jax import lax
from jax.experimental import pallas as pl
from jax.experimental.pallas import tpu as pltpu
from jax.sharding import PartitionSpec as P

TAPS = 7
MESH = pl.DeviceIdType.MESH
ROWS = 128
HALO = 8
PAD = 16
DEPTH = 512
CH = 512
NCTX = 16
NZ = 4
PART = CH // NCTX
SUB = 32
F32 = jnp.float32
BF16 = jnp.bfloat16


def split(table):
    high = table.astype(ml_dtypes.bfloat16)
    low = (table - high.astype(np.float64)).astype(ml_dtypes.bfloat16)
    return high, low


def tables():
    size = 2 * ROWS
    time = np.arange(ROWS)[:, None]
    freq = np.arange(ROWS)[None, :]
    angle = 2 * np.pi * (time * freq % size) / size
    imag = -np.sin(angle)
    imag[:, 0] = np.where(np.arange(ROWS) % 2 == 0, 1.0, -1.0)
    forward = np.concatenate([np.cos(angle), imag], 1)
    weight = np.where(np.arange(ROWS) == 0, 1.0, 2.0)[None, :] / size
    back_real = np.cos(angle) * weight
    back_imag = -np.sin(angle) * weight
    back_imag[:, 0] = np.where(np.arange(ROWS) % 2 == 0, 1.0, -1.0) / size
    inverse = np.concatenate([back_real, back_imag], 1).T
    return (*split(forward), *split(inverse))


def nt_dot(left, right):
    return lax.dot_general(left, right, (((1,), (1,)), ((), ())), preferred_element_type=F32)


def dot(left, right):
    return jnp.dot(left, right, preferred_element_type=F32)


def eye(rows, columns, offset):
    row = lax.broadcasted_iota(jnp.int32, (rows, columns), 0)
    column = lax.broadcasted_iota(jnp.int32, (rows, columns), 1)
    return row + offset == column


def kernel(
    tokens, weight, taps, filters, skip, fwd_hi, fwd_lo, inv_hi, inv_lo, out,
    slots, w_v, taps_v, filt_v, skip_v, fh_v, fl_v, ih_v, il_v,
    total, ext, gate, filt_t, spec, gain_re, gain_im, gain_ny, psend, precv, yhat, ysend, yrecv,
    w_sem, load_sem, own_sem, g_send, g_recv, h_send, h_recv, p_send, p_recv, y_send, y_recv, ready,
):
    ctx = lax.axis_index("ctx")
    tp = lax.axis_index("tp")
    y, z = tp // NZ, tp % NZ
    y_side = (1 - y) * NZ + z
    z_up = y * NZ + (z + 1) % NZ
    z_down = y * NZ + (z + NZ - 1) % NZ

    def peer(mask):
        other = ctx
        for bit in (1, 2, 4, 8):
            if mask & bit:
                other = other + bit * (1 - 2 * ((ctx // bit) % 2))
        return other

    for index in range(2 * NZ):
        slots[index, pl.ds(0, PAD)] = jnp.zeros((PAD, DEPTH), BF16)

    barrier = pltpu.get_barrier_semaphore()
    for side in (y_side, z_up, z_down):
        pl.semaphore_signal(barrier, inc=1, device_id={"ctx": ctx, "tp": side}, device_id_type=MESH)
    beside = (ctx + jnp.where(ctx % 2 == 0, NCTX - 1, 1)) % NCTX
    for other in (peer(1), peer(2), peer(4), peer(8), beside):
        pl.semaphore_signal(barrier, inc=1, device_id={"ctx": other, "tp": tp}, device_id_type=MESH)

    def tell(turn):
        pl.semaphore_signal(
            ready.at[turn], inc=1, device_id={"ctx": peer(1 << turn), "tp": tp}, device_id_type=MESH
        )

    def hear(turn):
        pl.semaphore_wait(ready.at[turn], 1)

    loads = [
        pltpu.make_async_copy(src, dst, load_sem.at[index])
        for index, (src, dst) in enumerate(
            [
                (filters.at[:, pl.ds(pl.multiple_of(ctx // 4 * 128, 128), 128)], filt_v),
                (fwd_hi, fh_v),
                (fwd_lo, fl_v),
                (inv_hi, ih_v),
                (inv_lo, il_v),
                (taps, taps_v),
                (skip, skip_v),
            ]
        )
    ]
    own = pltpu.make_async_copy(tokens, slots.at[0, pl.ds(PAD, ROWS)], own_sem.at[0])
    own.start()
    for load in loads:
        load.start()

    def source(dy, dz):
        there = (1 - y) if dy else y
        return there * NZ + (z + dz) % NZ

    def weight_load(dy, dz):
        rows = pl.ds(pl.multiple_of(source(dy, dz) * DEPTH, DEPTH), DEPTH)
        return pltpu.make_async_copy(weight.at[:, rows], w_v.at[:, rows], w_sem.at[dy * NZ + dz])

    order = [(0, 0), (1, 0), (0, 3), (0, 1), (0, 2), (1, 3), (1, 1), (1, 2)]
    for dy, dz in order:
        weight_load(dy, dz).start()

    pl.semaphore_wait(barrier, 8)

    def rows_of(piece):
        return pl.ds(PAD + piece * SUB, SUB)

    pieces = ROWS // SUB
    low = list(range(pieces // 2))
    high = list(range(pieces // 2, pieces))

    def gather_copy(src_slot, piece, dst_slot, side):
        first = src_slot == (0, 0)
        src = tokens.at[pl.ds(piece * SUB, SUB)] if first else slots.at[src_slot[0] * NZ + src_slot[1], rows_of(piece)]
        index = dst_slot[0] * NZ + dst_slot[1]
        return pltpu.make_async_remote_copy(
            src_ref=src,
            dst_ref=slots.at[index, rows_of(piece)],
            send_sem=g_send.at[index, piece],
            recv_sem=g_recv.at[index, piece],
            device_id={"ctx": ctx, "tp": side},
            device_id_type=MESH,
        )

    sent = []

    def send(src_slot, piece, dst_slot, side):
        copy = gather_copy(src_slot, piece, dst_slot, side)
        copy.start()
        sent.append(copy)

    def arrived(slot, piece):
        gather_copy((1, 1), piece, slot, z_up).wait_recv()

    halo_rows = pl.ds(PAD - HALO, HALO)

    def halo_copy(src_slot, dst_slot, device):
        index = dst_slot[0] * NZ + dst_slot[1]
        src = slots.at[src_slot[0] * NZ + src_slot[1], halo_rows]
        if dst_slot == (0, 0):
            src = tokens.at[pl.ds(ROWS - HALO, HALO)]
        return pltpu.make_async_remote_copy(
            src_ref=src,
            dst_ref=slots.at[index, halo_rows],
            send_sem=h_send.at[index],
            recv_sem=h_recv.at[index],
            device_id=device,
            device_id_type=MESH,
        )

    @pl.when(ctx < NCTX - 1)
    def _():
        halo_copy((0, 0), (0, 0), {"ctx": ctx + 1, "tp": tp}).start()

    for a, b in zip(high, low):
        send((0, 0), a, (1, 0), y_side)
        send((0, 0), a, (0, 3), z_up)
        send((0, 0), b, (0, 1), z_down)
        send((0, 0), b, (1, 0), y_side)
    for a, b in zip(high, low):
        send((0, 0), b, (0, 3), z_up)
        send((0, 0), a, (0, 1), z_down)

    halo_hops = [
        ((0, 0), (1, 0), y_side),
        ((0, 0), (0, 3), z_up),
        ((0, 0), (0, 1), z_down),
        ((0, 3), (0, 2), z_up),
        ((1, 0), (1, 3), z_up),
        ((1, 0), (1, 1), z_down),
        ((1, 3), (1, 2), z_up),
    ]

    def halo_arrived(slot):
        halo_copy((0, 1), slot, {"ctx": ctx, "tp": z_up}).wait_recv()

    def halo_from(slot):
        for src, dst, side in halo_hops:
            if src == slot:
                halo_copy(src, dst, {"ctx": ctx, "tp": side}).start()

    def halo_step(slot):
        @pl.when(ctx > 0)
        def _():
            halo_arrived(slot)
            halo_from(slot)

    tell(0)

    for load in loads:
        load.wait()
    pick = eye(PART, 128, ctx % 4 * PART)
    across = nt_dot(pick.astype(BF16), filt_v[...]).astype(BF16)
    for block in range(NCTX):
        filt_t[pl.ds(block * PART, PART)] = across[:, block * ROWS : (block + 1) * ROWS]
    spec[...] = dot(filt_t[...], fh_v[...]) + dot(filt_t[...], fl_v[...])
    lane = lax.broadcasted_iota(jnp.int32, (PART, ROWS), 1)
    swap = jnp.where(lane % 2 == 0, 1.0, -1.0).astype(F32)
    first_lane = lane == 0
    for block in range(NCTX):
        now = pl.ds(block * PART, PART)
        real = spec[now, :ROWS]
        imag = spec[now, ROWS:]
        if block:
            before = pl.ds((block - 1) * PART, PART)
            real = real + swap * spec[before, :ROWS]
            imag = imag + swap * spec[before, ROWS:]
        gain_re[now] = real
        gain_im[now] = jnp.where(first_lane, 0.0, imag)
        gain_ny[now] = jnp.where(first_lane, imag, real)

    own.wait()
    halo_step((0, 0))

    def project(slot, start):
        weight_load(*slot).wait()
        index = slot[0] * NZ + slot[1]
        rows = pl.ds(pl.multiple_of(source(*slot) * DEPTH, DEPTH), DEPTH)

        def branch(b, carry):
            term = dot(slots[index], w_v[b, rows])
            total[b] = term if start else total[b] + term
            return carry

        lax.fori_loop(0, 3, branch, 0)

    hear(0)
    tell(1)
    project((0, 0), True)

    for a, b in zip(high, low):
        arrived((1, 0), a)
        send((1, 0), a, (1, 3), z_up)
        arrived((0, 1), b)
        send((0, 1), b, (0, 2), z_down)
        arrived((0, 3), a)
        send((0, 3), a, (0, 2), z_up)
        arrived((1, 0), b)
        send((1, 0), b, (1, 1), z_down)
    hear(1)
    tell(2)
    halo_step((1, 0))
    project((1, 0), False)
    for a, b in zip(high, low):
        arrived((0, 3), b)
        send((0, 3), b, (1, 3), y_side)
        arrived((0, 1), a)
        send((0, 1), a, (1, 1), y_side)
    halo_step((0, 3))
    halo_step((0, 1))
    project((0, 3), False)
    for a, b in zip(high, low):
        arrived((1, 3), a)
        send((1, 3), a, (1, 2), z_up)
        arrived((1, 1), b)
        send((1, 1), b, (1, 2), z_down)
    halo_step((1, 3))
    project((0, 1), False)
    for piece in range(pieces):
        arrived((0, 2), piece)
    halo_step((0, 2))
    project((0, 2), False)
    for piece in low:
        arrived((1, 3), piece)
    project((1, 3), False)
    for piece in high:
        arrived((1, 1), piece)
    halo_step((1, 1))
    project((1, 1), False)
    for piece in range(pieces):
        arrived((1, 2), piece)
    halo_step((1, 2))
    project((1, 2), False)

    hear(2)

    def message(send_buffer, recv_buffer, send_sem, recv_sem, mask):
        other = peer(mask)
        copy = pltpu.make_async_remote_copy(
            src_ref=send_buffer.at[other],
            dst_ref=recv_buffer.at[ctx],
            send_sem=send_sem.at[mask],
            recv_sem=recv_sem.at[mask],
            device_id={"ctx": other, "tp": tp},
            device_id_type=MESH,
        )
        copy.start()
        return copy

    ident = eye(ROWS, ROWS, 0).astype(BF16)
    per = 128 // PART
    copies = []
    for far, near in ((3, (0, 1, 2, 3)), (2, (2, 3, 0, 1)), (1, (0, 1, 2, 3)), (0, (2, 3, 1))):
        quad = peer(far * per) // per
        lanes = pl.ds(pl.multiple_of(quad * 128, 128), 128)
        branches = []
        for b in range(3):
            ext[b] = total[b, :, lanes].astype(BF16).astype(F32)
            acc = taps_v[b, pl.ds(0, 1), lanes] * ext[b, pl.ds(PAD - TAPS + 1, ROWS)]
            for t in range(1, TAPS):
                acc = acc + taps_v[b, pl.ds(t, 1), lanes] * ext[b, pl.ds(PAD - TAPS + 1 + t, ROWS)]
            branches.append(acc)
        gate[:, lanes] = branches[0]
        product = (branches[1] * branches[2]).astype(BF16)
        turned = nt_dot(ident, product).astype(BF16)
        psend[pl.ds(quad * per, per)] = turned.reshape(per, PART, ROWS)
        for low_mask in near:
            copies.append(message(psend, precv, p_send, p_recv, far * per + low_mask))
    precv[pl.ds(ctx, 1)] = psend[pl.ds(ctx, 1)]
    for copy in copies:
        copy.wait()

    block_rows = precv[...].reshape(NCTX * PART, ROWS)
    spec[...] = dot(block_rows, fh_v[...]) + dot(block_rows, fl_v[...])
    for block in range(NCTX):
        real = jnp.zeros((PART, ROWS), F32)
        imag = jnp.zeros((PART, ROWS), F32)
        for earlier in range(block + 1):
            lag = pl.ds((block - earlier) * PART, PART)
            src = pl.ds(earlier * PART, PART)
            p_real = spec[src, :ROWS]
            p_imag = spec[src, ROWS:]
            cross = gain_im[lag]
            real = real + gain_re[lag] * p_real - cross * p_imag
            imag = imag + gain_ny[lag] * p_imag + cross * p_real
        now = pl.ds(block * PART, PART)
        yhat[now, :ROWS] = real
        yhat[now, ROWS:] = imag
    both = yhat[...]
    upper = both.astype(BF16)
    lower = (both - upper.astype(F32)).astype(BF16)
    convolved = dot(upper, ih_v[...]) + dot(upper, il_v[...]) + dot(lower, ih_v[...])
    skip_row = skip_v[:, pl.ds(pl.multiple_of(ctx // 4 * 128, 128), 128)]
    skip_column = jnp.sum(jnp.where(pick, skip_row, 0.0), axis=1, keepdims=True)
    direct = skip_column[None] * precv[...].astype(F32)
    ysend[...] = (convolved.reshape(NCTX, PART, ROWS) + direct).astype(BF16)

    far_first = [12, 13, 10, 11, 14, 15, 8, 9, 4, 5, 2, 3, 6, 7, 1]
    copies = [message(ysend, yrecv, y_send, y_recv, mask) for mask in far_first]
    yrecv[pl.ds(ctx, 1)] = ysend[pl.ds(ctx, 1)]
    for copy in copies:
        copy.wait()

    mixed = nt_dot(ident, yrecv[...].reshape(CH, ROWS))
    out[...] = (gate[...] * mixed).astype(BF16)

    for copy in sent:
        copy.wait_send()

    @pl.when(ctx < NCTX - 1)
    def _():
        halo_copy((0, 0), (0, 0), {"ctx": ctx + 1, "tp": tp}).wait_send()

    @pl.when(ctx > 0)
    def _():
        for src, dst, side in halo_hops:
            halo_copy(src, dst, {"ctx": ctx, "tp": side}).wait_send()


def local(tokens, in_weight, conv_weight, filters, skip_gain):
    any_space = pl.BlockSpec(memory_space=pl.ANY)
    dma = pltpu.SemaphoreType.DMA
    pieces = ROWS // SUB
    size = 2 * ROWS
    scratch = [
        pltpu.VMEM((2 * NZ, PAD + ROWS, DEPTH), BF16),
        pltpu.VMEM((3, 2 * NZ * DEPTH, CH), BF16),
        pltpu.VMEM((3, TAPS, CH), F32),
        pltpu.VMEM((NCTX * ROWS, 128), BF16),
        pltpu.VMEM((1, CH), F32),
        pltpu.VMEM((ROWS, size), BF16),
        pltpu.VMEM((ROWS, size), BF16),
        pltpu.VMEM((size, ROWS), BF16),
        pltpu.VMEM((size, ROWS), BF16),
        pltpu.VMEM((3, PAD + ROWS, CH), F32),
        pltpu.VMEM((3, PAD + ROWS, 128), F32),
        pltpu.VMEM((ROWS, CH), F32),
        pltpu.VMEM((NCTX * PART, ROWS), BF16),
        pltpu.VMEM((NCTX * PART, size), F32),
        pltpu.VMEM((NCTX * PART, ROWS), F32),
        pltpu.VMEM((NCTX * PART, ROWS), F32),
        pltpu.VMEM((NCTX * PART, ROWS), F32),
        pltpu.VMEM((NCTX, PART, ROWS), BF16),
        pltpu.VMEM((NCTX, PART, ROWS), BF16),
        pltpu.VMEM((NCTX * PART, size), F32),
        pltpu.VMEM((NCTX, PART, ROWS), BF16),
        pltpu.VMEM((NCTX, PART, ROWS), BF16),
        dma((2 * NZ,)),
        dma((7,)),
        dma((1,)),
        dma((2 * NZ, pieces)),
        dma((2 * NZ, pieces)),
        dma((2 * NZ,)),
        dma((2 * NZ,)),
        dma((NCTX,)),
        dma((NCTX,)),
        dma((NCTX,)),
        dma((NCTX,)),
        pltpu.SemaphoreType.REGULAR((3,)),
    ]
    return pl.pallas_call(
        kernel,
        out_shape=jax.ShapeDtypeStruct((ROWS, CH), BF16),
        in_specs=[any_space] * 9,
        out_specs=pl.BlockSpec(memory_space=pltpu.VMEM),
        scratch_shapes=scratch,
        compiler_params=pltpu.CompilerParams(
            collective_id=0, has_side_effects=True, vmem_limit_bytes=56 * 1024 * 1024
        ),
        name="hyena",
    )(
        tokens,
        jnp.transpose(in_weight, (1, 0, 2)),
        jnp.transpose(conv_weight, (1, 0, 2)),
        filters,
        skip_gain.reshape(1, CH),
        *(jnp.asarray(table) for table in tables()),
    )


def solution(mesh):
    placed = (P("ctx", "tp"), P(None, None, "tp"), P(None, None, "tp"), P(None, "tp"), P("tp"))
    return jax.shard_map(local, mesh=mesh, in_specs=placed, out_specs=P("ctx", "tp"), check_vma=False)
```

```python
import functools

import jax
import jax.numpy as jnp
import ml_dtypes
import numpy as np
from jax import lax
from jax.experimental import pallas as pl
from jax.experimental.pallas import tpu as pltpu
from jax.sharding import PartitionSpec as P

TAPS = 7
MESH = pl.DeviceIdType.MESH
ROWS = 128
HALO = 8
PAD = 16
DEPTH = 512
CH = 512
NCTX = 16
NZ = 4
PART = CH // NCTX
SUB = 32
F32 = jnp.float32
BF16 = jnp.bfloat16


def split(table):
    high = table.astype(ml_dtypes.bfloat16)
    low = (table - high.astype(np.float64)).astype(ml_dtypes.bfloat16)
    return high, low


def tables():
    size = 2 * ROWS
    time = np.arange(ROWS)[:, None]
    freq = np.arange(ROWS)[None, :]
    angle = 2 * np.pi * (time * freq % size) / size
    imag = -np.sin(angle)
    imag[:, 0] = np.where(np.arange(ROWS) % 2 == 0, 1.0, -1.0)
    forward = np.concatenate([np.cos(angle), imag], 1)
    weight = np.where(np.arange(ROWS) == 0, 1.0, 2.0)[None, :] / size
    back_real = np.cos(angle) * weight
    back_imag = -np.sin(angle) * weight
    back_imag[:, 0] = np.where(np.arange(ROWS) % 2 == 0, 1.0, -1.0) / size
    inverse = np.concatenate([back_real, back_imag], 1).T
    return (*split(forward), *split(inverse))


def nt_dot(left, right):
    return lax.dot_general(left, right, (((1,), (1,)), ((), ())), preferred_element_type=F32)


def dot(left, right):
    return jnp.dot(left, right, preferred_element_type=F32)


def eye(rows, columns, offset):
    row = lax.broadcasted_iota(jnp.int32, (rows, columns), 0)
    column = lax.broadcasted_iota(jnp.int32, (rows, columns), 1)
    return row + offset == column


def kernel(
    tokens, weight, taps, filters, skip, fwd_hi, fwd_lo, inv_hi, inv_lo, out,
    slots, w_v, taps_v, filt_v, skip_v, fh_v, fl_v, ih_v, il_v,
    total, ext, gate, filt_t, spec, gain_re, gain_im, gain_ny, psend, precv, yhat, ysend, yrecv,
    w_sem, load_sem, own_sem, g_send, g_recv, h_send, h_recv, p_send, p_recv, y_send, y_recv, ready,
):
    ctx = lax.axis_index("ctx")
    tp = lax.axis_index("tp")
    y, z = tp // NZ, tp % NZ
    y_side = (1 - y) * NZ + z
    z_up = y * NZ + (z + 1) % NZ
    z_down = y * NZ + (z + NZ - 1) % NZ

    def peer(mask):
        other = ctx
        for bit in (1, 2, 4, 8):
            if mask & bit:
                other = other + bit * (1 - 2 * ((ctx // bit) % 2))
        return other

    for index in range(2 * NZ):
        slots[index, pl.ds(0, PAD)] = jnp.zeros((PAD, DEPTH), BF16)

    barrier = pltpu.get_barrier_semaphore()
    for side in (y_side, z_up, z_down):
        pl.semaphore_signal(barrier, inc=1, device_id={"ctx": ctx, "tp": side}, device_id_type=MESH)
    beside = (ctx + jnp.where(ctx % 2 == 0, NCTX - 1, 1)) % NCTX
    for other in (peer(1), peer(2), peer(4), peer(8), beside):
        pl.semaphore_signal(barrier, inc=1, device_id={"ctx": other, "tp": tp}, device_id_type=MESH)

    def tell(turn):
        pl.semaphore_signal(
            ready.at[turn], inc=1, device_id={"ctx": peer(1 << turn), "tp": tp}, device_id_type=MESH
        )

    def hear(turn):
        pl.semaphore_wait(ready.at[turn], 1)

    loads = [
        pltpu.make_async_copy(src, dst, load_sem.at[index])
        for index, (src, dst) in enumerate(
            [
                (filters.at[:, pl.ds(pl.multiple_of(ctx // 4 * 128, 128), 128)], filt_v),
                (fwd_hi, fh_v),
                (fwd_lo, fl_v),
                (inv_hi, ih_v),
                (inv_lo, il_v),
                (taps, taps_v),
                (skip, skip_v),
            ]
        )
    ]
    own = pltpu.make_async_copy(tokens, slots.at[0, pl.ds(PAD, ROWS)], own_sem.at[0])
    own.start()
    for load in loads:
        load.start()

    def source(dy, dz):
        there = (1 - y) if dy else y
        return there * NZ + (z + dz) % NZ

    def weight_load(dy, dz):
        rows = pl.ds(pl.multiple_of(source(dy, dz) * DEPTH, DEPTH), DEPTH)
        return pltpu.make_async_copy(weight.at[:, rows], w_v.at[:, rows], w_sem.at[dy * NZ + dz])

    order = [(0, 0), (1, 0), (0, 3), (0, 1), (0, 2), (1, 3), (1, 1), (1, 2)]
    for dy, dz in order:
        weight_load(dy, dz).start()

    pl.semaphore_wait(barrier, 8)

    def rows_of(piece):
        return pl.ds(PAD + piece * SUB, SUB)

    pieces = ROWS // SUB
    low = list(range(pieces // 2))
    high = list(range(pieces // 2, pieces))

    def gather_copy(src_slot, piece, dst_slot, side):
        first = src_slot == (0, 0)
        src = tokens.at[pl.ds(piece * SUB, SUB)] if first else slots.at[src_slot[0] * NZ + src_slot[1], rows_of(piece)]
        index = dst_slot[0] * NZ + dst_slot[1]
        return pltpu.make_async_remote_copy(
            src_ref=src,
            dst_ref=slots.at[index, rows_of(piece)],
            send_sem=g_send.at[index, piece],
            recv_sem=g_recv.at[index, piece],
            device_id={"ctx": ctx, "tp": side},
            device_id_type=MESH,
        )

    sent = []

    def send(src_slot, piece, dst_slot, side):
        copy = gather_copy(src_slot, piece, dst_slot, side)
        copy.start()
        sent.append(copy)

    def arrived(slot, piece):
        gather_copy((1, 1), piece, slot, z_up).wait_recv()

    halo_rows = pl.ds(PAD - HALO, HALO)

    def halo_copy(src_slot, dst_slot, device):
        index = dst_slot[0] * NZ + dst_slot[1]
        src = slots.at[src_slot[0] * NZ + src_slot[1], halo_rows]
        if dst_slot == (0, 0):
            src = tokens.at[pl.ds(ROWS - HALO, HALO)]
        return pltpu.make_async_remote_copy(
            src_ref=src,
            dst_ref=slots.at[index, halo_rows],
            send_sem=h_send.at[index],
            recv_sem=h_recv.at[index],
            device_id=device,
            device_id_type=MESH,
        )

    @pl.when(ctx < NCTX - 1)
    def _():
        halo_copy((0, 0), (0, 0), {"ctx": ctx + 1, "tp": tp}).start()

    for a, b in zip(high, low):
        send((0, 0), a, (1, 0), y_side)
        send((0, 0), a, (0, 3), z_up)
        send((0, 0), b, (0, 1), z_down)
        send((0, 0), b, (1, 0), y_side)
    for a, b in zip(high, low):
        send((0, 0), b, (0, 3), z_up)
        send((0, 0), a, (0, 1), z_down)

    halo_hops = [
        ((0, 0), (1, 0), y_side),
        ((0, 0), (0, 3), z_up),
        ((0, 0), (0, 1), z_down),
        ((0, 3), (0, 2), z_up),
        ((1, 0), (1, 3), z_up),
        ((1, 0), (1, 1), z_down),
        ((1, 3), (1, 2), z_up),
    ]

    def halo_arrived(slot):
        halo_copy((0, 1), slot, {"ctx": ctx, "tp": z_up}).wait_recv()

    def halo_from(slot):
        for src, dst, side in halo_hops:
            if src == slot:
                halo_copy(src, dst, {"ctx": ctx, "tp": side}).start()

    def halo_step(slot):
        @pl.when(ctx > 0)
        def _():
            halo_arrived(slot)
            halo_from(slot)

    tell(0)

    for load in loads:
        load.wait()
    pick = eye(PART, 128, ctx % 4 * PART)
    across = nt_dot(pick.astype(BF16), filt_v[...]).astype(BF16)
    for block in range(NCTX):
        filt_t[pl.ds(block * PART, PART)] = across[:, block * ROWS : (block + 1) * ROWS]
    spec[...] = dot(filt_t[...], fh_v[...]) + dot(filt_t[...], fl_v[...])
    lane = lax.broadcasted_iota(jnp.int32, (PART, ROWS), 1)
    swap = jnp.where(lane % 2 == 0, 1.0, -1.0).astype(F32)
    first_lane = lane == 0
    for block in range(NCTX):
        now = pl.ds(block * PART, PART)
        real = spec[now, :ROWS]
        imag = spec[now, ROWS:]
        if block:
            before = pl.ds((block - 1) * PART, PART)
            real = real + swap * spec[before, :ROWS]
            imag = imag + swap * spec[before, ROWS:]
        gain_re[now] = real
        gain_im[now] = jnp.where(first_lane, 0.0, imag)
        gain_ny[now] = jnp.where(first_lane, imag, real)

    own.wait()
    halo_step((0, 0))

    def project(slot, start):
        weight_load(*slot).wait()
        index = slot[0] * NZ + slot[1]
        rows = pl.ds(pl.multiple_of(source(*slot) * DEPTH, DEPTH), DEPTH)

        def branch(b, carry):
            term = dot(slots[index], w_v[b, rows])
            total[b] = term if start else total[b] + term
            return carry

        lax.fori_loop(0, 3, branch, 0)

    hear(0)
    tell(1)
    project((0, 0), True)

    for a, b in zip(high, low):
        arrived((1, 0), a)
        send((1, 0), a, (1, 3), z_up)
        arrived((0, 1), b)
        send((0, 1), b, (0, 2), z_down)
        arrived((0, 3), a)
        send((0, 3), a, (0, 2), z_up)
        arrived((1, 0), b)
        send((1, 0), b, (1, 1), z_down)
    hear(1)
    tell(2)
    halo_step((1, 0))
    project((1, 0), False)
    for a, b in zip(high, low):
        arrived((0, 3), b)
        send((0, 3), b, (1, 3), y_side)
        arrived((0, 1), a)
        send((0, 1), a, (1, 1), y_side)
    halo_step((0, 3))
    halo_step((0, 1))
    project((0, 3), False)
    for a, b in zip(high, low):
        arrived((1, 3), a)
        send((1, 3), a, (1, 2), z_up)
        arrived((1, 1), b)
        send((1, 1), b, (1, 2), z_down)
    halo_step((1, 3))
    project((0, 1), False)
    for piece in range(pieces):
        arrived((0, 2), piece)
    halo_step((0, 2))
    project((0, 2), False)
    for piece in low:
        arrived((1, 3), piece)
    project((1, 3), False)
    for piece in high:
        arrived((1, 1), piece)
    halo_step((1, 1))
    project((1, 1), False)
    for piece in range(pieces):
        arrived((1, 2), piece)
    halo_step((1, 2))
    project((1, 2), False)

    hear(2)

    def message(send_buffer, recv_buffer, send_sem, recv_sem, mask):
        other = peer(mask)
        return pltpu.make_async_remote_copy(
            src_ref=send_buffer.at[other],
            dst_ref=recv_buffer.at[ctx],
            send_sem=send_sem.at[mask],
            recv_sem=recv_sem.at[mask],
            device_id={"ctx": other, "tp": tp},
            device_id_type=MESH,
        )

    def p_message(mask):
        return message(psend, precv, p_send, p_recv, mask)

    def y_message(mask):
        return message(ysend, yrecv, y_send, y_recv, mask)

    ident = eye(ROWS, ROWS, 0).astype(BF16)
    per = 128 // PART
    for far, near in ((3, (0, 1, 2, 3)), (2, (2, 3, 0, 1)), (1, (0, 1, 2, 3)), (0, (2, 3, 1))):
        quad = peer(far * per) // per
        lanes = pl.ds(pl.multiple_of(quad * 128, 128), 128)
        branches = []
        for b in range(3):
            ext[b] = total[b, :, lanes].astype(BF16).astype(F32)
            acc = taps_v[b, pl.ds(0, 1), lanes] * ext[b, pl.ds(PAD - TAPS + 1, ROWS)]
            for t in range(1, TAPS):
                acc = acc + taps_v[b, pl.ds(t, 1), lanes] * ext[b, pl.ds(PAD - TAPS + 1 + t, ROWS)]
            branches.append(acc)
        gate[:, lanes] = branches[0]
        product = (branches[1] * branches[2]).astype(BF16)
        turned = nt_dot(ident, product).astype(BF16)
        psend[pl.ds(quad * per, per)] = turned.reshape(per, PART, ROWS)
        for low_mask in near:
            p_message(far * per + low_mask).start()
    precv[pl.ds(ctx, 1)] = psend[pl.ds(ctx, 1)]

    half_blocks = NCTX // 2
    near_masks = [4, 5, 2, 3, 6, 7, 1]
    far_masks = [12, 13, 10, 11, 14, 15, 8, 9]
    skip_row = skip_v[:, pl.ds(pl.multiple_of(ctx // 4 * 128, 128), 128)]
    skip_column = jnp.sum(jnp.where(pick, skip_row, 0.0), axis=1, keepdims=True)

    def blocks_of(half):
        return pl.ds(half * half_blocks, half_blocks)

    def rows_in(half):
        return pl.ds(half * half_blocks * PART, half_blocks * PART)

    def forward(half):
        block_rows = precv[blocks_of(half)].reshape(half_blocks * PART, ROWS)
        spec[rows_in(half)] = dot(block_rows, fh_v[...]) + dot(block_rows, fl_v[...])

    def gather_terms(to_half, from_half, start):
        for block in range(to_half * half_blocks, (to_half + 1) * half_blocks):
            now = pl.ds(block * PART, PART)
            real = jnp.zeros((PART, ROWS), F32) if start else yhat[now, :ROWS]
            imag = jnp.zeros((PART, ROWS), F32) if start else yhat[now, ROWS:]
            for earlier in range(from_half * half_blocks, min(block + 1, (from_half + 1) * half_blocks)):
                lag = pl.ds((block - earlier) * PART, PART)
                src = pl.ds(earlier * PART, PART)
                p_real = spec[src, :ROWS]
                p_imag = spec[src, ROWS:]
                cross = gain_im[lag]
                real = real + gain_re[lag] * p_real - cross * p_imag
                imag = imag + gain_ny[lag] * p_imag + cross * p_real
            yhat[now, :ROWS] = real
            yhat[now, ROWS:] = imag

    def finish(half, masks):
        both = yhat[rows_in(half)]
        upper = both.astype(BF16)
        lower = (both - upper.astype(F32)).astype(BF16)
        convolved = dot(upper, ih_v[...]) + dot(upper, il_v[...]) + dot(lower, ih_v[...])
        direct = skip_column[None] * precv[blocks_of(half)].astype(F32)
        ysend[blocks_of(half)] = (convolved.reshape(half_blocks, PART, ROWS) + direct).astype(BF16)
        for mask in masks:
            y_message(mask).start()

    for mask in near_masks:
        p_message(mask).wait_recv()

    @pl.when(ctx < half_blocks)
    def _():
        forward(0)
        gather_terms(0, 0, True)
        gather_terms(1, 0, True)
        for mask in far_masks:
            p_message(mask).wait_recv()
        forward(1)
        gather_terms(1, 1, False)
        finish(1, far_masks)
        finish(0, near_masks)

    @pl.when(ctx >= half_blocks)
    def _():
        forward(1)
        gather_terms(1, 1, True)
        for mask in far_masks:
            p_message(mask).wait_recv()
        forward(0)
        gather_terms(0, 0, True)
        finish(0, far_masks)
        gather_terms(1, 0, False)
        finish(1, near_masks)

    yrecv[pl.ds(ctx, 1)] = ysend[pl.ds(ctx, 1)]

    def mix(half, masks):
        for mask in masks:
            y_message(mask).wait_recv()
        lanes = pl.ds(pl.multiple_of(half * (CH // 2), CH // 2), CH // 2)
        mixed = nt_dot(ident, yrecv[blocks_of(half)].reshape(CH // 2, ROWS))
        out[:, lanes] = (gate[:, lanes] * mixed).astype(BF16)

    own_half = ctx // half_blocks
    mix(own_half, near_masks)
    mix(1 - own_half, far_masks)

    for mask in near_masks + far_masks:
        p_message(mask).wait_send()
        y_message(mask).wait_send()
    for copy in sent:
        copy.wait_send()

    @pl.when(ctx < NCTX - 1)
    def _():
        halo_copy((0, 0), (0, 0), {"ctx": ctx + 1, "tp": tp}).wait_send()

    @pl.when(ctx > 0)
    def _():
        for src, dst, side in halo_hops:
            halo_copy(src, dst, {"ctx": ctx, "tp": side}).wait_send()


def local(tokens, in_weight, conv_weight, filters, skip_gain):
    any_space = pl.BlockSpec(memory_space=pl.ANY)
    dma = pltpu.SemaphoreType.DMA
    pieces = ROWS // SUB
    size = 2 * ROWS
    scratch = [
        pltpu.VMEM((2 * NZ, PAD + ROWS, DEPTH), BF16),
        pltpu.VMEM((3, 2 * NZ * DEPTH, CH), BF16),
        pltpu.VMEM((3, TAPS, CH), F32),
        pltpu.VMEM((NCTX * ROWS, 128), BF16),
        pltpu.VMEM((1, CH), F32),
        pltpu.VMEM((ROWS, size), BF16),
        pltpu.VMEM((ROWS, size), BF16),
        pltpu.VMEM((size, ROWS), BF16),
        pltpu.VMEM((size, ROWS), BF16),
        pltpu.VMEM((3, PAD + ROWS, CH), F32),
        pltpu.VMEM((3, PAD + ROWS, 128), F32),
        pltpu.VMEM((ROWS, CH), F32),
        pltpu.VMEM((NCTX * PART, ROWS), BF16),
        pltpu.VMEM((NCTX * PART, size), F32),
        pltpu.VMEM((NCTX * PART, ROWS), F32),
        pltpu.VMEM((NCTX * PART, ROWS), F32),
        pltpu.VMEM((NCTX * PART, ROWS), F32),
        pltpu.VMEM((NCTX, PART, ROWS), BF16),
        pltpu.VMEM((NCTX, PART, ROWS), BF16),
        pltpu.VMEM((NCTX * PART, size), F32),
        pltpu.VMEM((NCTX, PART, ROWS), BF16),
        pltpu.VMEM((NCTX, PART, ROWS), BF16),
        dma((2 * NZ,)),
        dma((7,)),
        dma((1,)),
        dma((2 * NZ, pieces)),
        dma((2 * NZ, pieces)),
        dma((2 * NZ,)),
        dma((2 * NZ,)),
        dma((NCTX,)),
        dma((NCTX,)),
        dma((NCTX,)),
        dma((NCTX,)),
        pltpu.SemaphoreType.REGULAR((3,)),
    ]
    return pl.pallas_call(
        kernel,
        out_shape=jax.ShapeDtypeStruct((ROWS, CH), BF16),
        in_specs=[any_space] * 9,
        out_specs=pl.BlockSpec(memory_space=pltpu.VMEM),
        scratch_shapes=scratch,
        compiler_params=pltpu.CompilerParams(
            collective_id=0, has_side_effects=True, vmem_limit_bytes=56 * 1024 * 1024
        ),
        name="hyena",
    )(
        tokens,
        jnp.transpose(in_weight, (1, 0, 2)),
        jnp.transpose(conv_weight, (1, 0, 2)),
        filters,
        skip_gain.reshape(1, CH),
        *(jnp.asarray(table) for table in tables()),
    )


def solution(mesh):
    placed = (P("ctx", "tp"), P(None, None, "tp"), P(None, None, "tp"), P(None, "tp"), P("tp"))
    return jax.shard_map(local, mesh=mesh, in_specs=placed, out_specs=P("ctx", "tp"), check_vma=False)
```

```python
import functools

import jax
import jax.numpy as jnp
import ml_dtypes
import numpy as np
from jax import lax
from jax.experimental import pallas as pl
from jax.experimental.pallas import tpu as pltpu
from jax.sharding import PartitionSpec as P

TAPS = 7
MESH = pl.DeviceIdType.MESH
ROWS = 128
HALO = 8
PAD = 16
DEPTH = 512
CH = 512
NCTX = 16
NZ = 4
PART = CH // NCTX
SUB = 32
F32 = jnp.float32
BF16 = jnp.bfloat16


def split(table):
    high = table.astype(ml_dtypes.bfloat16)
    low = (table - high.astype(np.float64)).astype(ml_dtypes.bfloat16)
    return high, low


def tables():
    size = 2 * ROWS
    time = np.arange(ROWS)[:, None]
    freq = np.arange(ROWS)[None, :]
    angle = 2 * np.pi * (time * freq % size) / size
    imag = -np.sin(angle)
    imag[:, 0] = np.where(np.arange(ROWS) % 2 == 0, 1.0, -1.0)
    forward = np.concatenate([np.cos(angle), imag], 1)
    weight = np.where(np.arange(ROWS) == 0, 1.0, 2.0)[None, :] / size
    back_real = np.cos(angle) * weight
    back_imag = -np.sin(angle) * weight
    back_imag[:, 0] = np.where(np.arange(ROWS) % 2 == 0, 1.0, -1.0) / size
    inverse = np.concatenate([back_real, back_imag], 1).T
    return (*split(forward), *split(inverse))


def nt_dot(left, right):
    return lax.dot_general(left, right, (((1,), (1,)), ((), ())), preferred_element_type=F32)


def dot(left, right):
    return jnp.dot(left, right, preferred_element_type=F32)


def eye(rows, columns, offset):
    row = lax.broadcasted_iota(jnp.int32, (rows, columns), 0)
    column = lax.broadcasted_iota(jnp.int32, (rows, columns), 1)
    return row + offset == column


def kernel(
    tokens, weight, taps, filters, skip, fwd_hi, fwd_lo, inv_hi, inv_lo, out,
    slots, w_v, taps_v, filt_v, skip_v, fh_v, fl_v, ih_v, il_v,
    total, ext, gate, filt_t, spec, gain_re, gain_im, gain_ny, psend, precv, yhat, ysend, yrecv,
    w_sem, load_sem, own_sem, g_send, g_recv, h_send, h_recv, p_send, p_recv, y_send, y_recv, ready,
):
    ctx = lax.axis_index("ctx")
    tp = lax.axis_index("tp")
    y, z = tp // NZ, tp % NZ
    y_side = (1 - y) * NZ + z
    z_up = y * NZ + (z + 1) % NZ
    z_down = y * NZ + (z + NZ - 1) % NZ

    def peer(mask):
        other = ctx
        for bit in (1, 2, 4, 8):
            if mask & bit:
                other = other + bit * (1 - 2 * ((ctx // bit) % 2))
        return other

    for index in range(2 * NZ):
        slots[index, pl.ds(0, PAD)] = jnp.zeros((PAD, DEPTH), BF16)

    barrier = pltpu.get_barrier_semaphore()
    for side in (y_side, z_up, z_down):
        pl.semaphore_signal(barrier, inc=1, device_id={"ctx": ctx, "tp": side}, device_id_type=MESH)
    beside = (ctx + jnp.where(ctx % 2 == 0, NCTX - 1, 1)) % NCTX
    for other in (peer(1), peer(2), peer(4), peer(8), beside):
        pl.semaphore_signal(barrier, inc=1, device_id={"ctx": other, "tp": tp}, device_id_type=MESH)

    def tell(turn):
        pl.semaphore_signal(
            ready.at[turn], inc=1, device_id={"ctx": peer(1 << turn), "tp": tp}, device_id_type=MESH
        )

    def hear(turn):
        pl.semaphore_wait(ready.at[turn], 1)

    loads = [
        pltpu.make_async_copy(src, dst, load_sem.at[index])
        for index, (src, dst) in enumerate(
            [
                (filters.at[:, pl.ds(pl.multiple_of(ctx // 4 * 128, 128), 128)], filt_v),
                (fwd_hi, fh_v),
                (fwd_lo, fl_v),
                (inv_hi, ih_v),
                (inv_lo, il_v),
                (taps, taps_v),
                (skip, skip_v),
            ]
        )
    ]
    own = pltpu.make_async_copy(tokens, slots.at[0, pl.ds(PAD, ROWS)], own_sem.at[0])
    own.start()
    for load in loads:
        load.start()

    def source(dy, dz):
        there = (1 - y) if dy else y
        return there * NZ + (z + dz) % NZ

    def weight_load(dy, dz):
        rows = pl.ds(pl.multiple_of(source(dy, dz) * DEPTH, DEPTH), DEPTH)
        return pltpu.make_async_copy(weight.at[:, rows], w_v.at[:, rows], w_sem.at[dy * NZ + dz])

    order = [(0, 0), (1, 0), (0, 3), (0, 1), (0, 2), (1, 3), (1, 1), (1, 2)]
    for dy, dz in order:
        weight_load(dy, dz).start()

    pl.semaphore_wait(barrier, 8)

    def rows_of(piece):
        return pl.ds(PAD + piece * SUB, SUB)

    pieces = ROWS // SUB
    low = list(range(pieces // 2))
    high = list(range(pieces // 2, pieces))

    def gather_copy(src_slot, piece, dst_slot, side):
        first = src_slot == (0, 0)
        src = tokens.at[pl.ds(piece * SUB, SUB)] if first else slots.at[src_slot[0] * NZ + src_slot[1], rows_of(piece)]
        index = dst_slot[0] * NZ + dst_slot[1]
        return pltpu.make_async_remote_copy(
            src_ref=src,
            dst_ref=slots.at[index, rows_of(piece)],
            send_sem=g_send.at[index, piece],
            recv_sem=g_recv.at[index, piece],
            device_id={"ctx": ctx, "tp": side},
            device_id_type=MESH,
        )

    sent = []

    def send(src_slot, piece, dst_slot, side):
        copy = gather_copy(src_slot, piece, dst_slot, side)
        copy.start()
        sent.append(copy)

    def arrived(slot, piece):
        gather_copy((1, 1), piece, slot, z_up).wait_recv()

    halo_rows = pl.ds(PAD - HALO, HALO)

    def halo_copy(src_slot, dst_slot, device):
        index = dst_slot[0] * NZ + dst_slot[1]
        src = slots.at[src_slot[0] * NZ + src_slot[1], halo_rows]
        if dst_slot == (0, 0):
            src = tokens.at[pl.ds(ROWS - HALO, HALO)]
        return pltpu.make_async_remote_copy(
            src_ref=src,
            dst_ref=slots.at[index, halo_rows],
            send_sem=h_send.at[index],
            recv_sem=h_recv.at[index],
            device_id=device,
            device_id_type=MESH,
        )

    @pl.when(ctx < NCTX - 1)
    def _():
        halo_copy((0, 0), (0, 0), {"ctx": ctx + 1, "tp": tp}).start()

    for a, b in zip(high, low):
        send((0, 0), a, (1, 0), y_side)
        send((0, 0), a, (0, 3), z_up)
        send((0, 0), b, (0, 1), z_down)
        send((0, 0), b, (1, 0), y_side)
    for a, b in zip(high, low):
        send((0, 0), b, (0, 3), z_up)
        send((0, 0), a, (0, 1), z_down)

    halo_hops = [
        ((0, 0), (1, 0), y_side),
        ((0, 0), (0, 3), z_up),
        ((0, 0), (0, 1), z_down),
        ((0, 3), (0, 2), z_up),
        ((1, 0), (1, 3), z_up),
        ((1, 0), (1, 1), z_down),
        ((1, 3), (1, 2), z_up),
    ]

    def halo_arrived(slot):
        halo_copy((0, 1), slot, {"ctx": ctx, "tp": z_up}).wait_recv()

    def halo_from(slot):
        for src, dst, side in halo_hops:
            if src == slot:
                halo_copy(src, dst, {"ctx": ctx, "tp": side}).start()

    def halo_step(slot):
        @pl.when(ctx > 0)
        def _():
            halo_arrived(slot)
            halo_from(slot)

    tell(0)

    for load in loads:
        load.wait()
    pick = eye(PART, 128, ctx % 4 * PART)
    across = nt_dot(pick.astype(BF16), filt_v[...]).astype(BF16)
    for block in range(NCTX):
        filt_t[pl.ds(block * PART, PART)] = across[:, block * ROWS : (block + 1) * ROWS]
    spec[...] = dot(filt_t[...], fh_v[...]) + dot(filt_t[...], fl_v[...])
    lane = lax.broadcasted_iota(jnp.int32, (PART, ROWS), 1)
    swap = jnp.where(lane % 2 == 0, 1.0, -1.0).astype(F32)
    first_lane = lane == 0
    for block in range(NCTX):
        now = pl.ds(block * PART, PART)
        real = spec[now, :ROWS]
        imag = spec[now, ROWS:]
        if block:
            before = pl.ds((block - 1) * PART, PART)
            real = real + swap * spec[before, :ROWS]
            imag = imag + swap * spec[before, ROWS:]
        gain_re[now] = real
        gain_im[now] = jnp.where(first_lane, 0.0, imag)
        gain_ny[now] = jnp.where(first_lane, imag, real)

    own.wait()
    halo_step((0, 0))

    def project(slot, start):
        weight_load(*slot).wait()
        index = slot[0] * NZ + slot[1]
        rows = pl.ds(pl.multiple_of(source(*slot) * DEPTH, DEPTH), DEPTH)

        def branch(b, carry):
            term = dot(slots[index], w_v[b, rows])
            total[b] = term if start else total[b] + term
            return carry

        lax.fori_loop(0, 3, branch, 0)

    hear(0)
    tell(1)
    project((0, 0), True)

    for a, b in zip(high, low):
        arrived((1, 0), a)
        send((1, 0), a, (1, 3), z_up)
        arrived((0, 1), b)
        send((0, 1), b, (0, 2), z_down)
        arrived((0, 3), a)
        send((0, 3), a, (0, 2), z_up)
        arrived((1, 0), b)
        send((1, 0), b, (1, 1), z_down)
    hear(1)
    tell(2)
    halo_step((1, 0))
    project((1, 0), False)
    for a, b in zip(high, low):
        arrived((0, 3), b)
        send((0, 3), b, (1, 3), y_side)
        arrived((0, 1), a)
        send((0, 1), a, (1, 1), y_side)
    halo_step((0, 3))
    halo_step((0, 1))
    project((0, 3), False)
    for a, b in zip(high, low):
        arrived((1, 3), a)
        send((1, 3), a, (1, 2), z_up)
        arrived((1, 1), b)
        send((1, 1), b, (1, 2), z_down)
    halo_step((1, 3))
    project((0, 1), False)
    for piece in range(pieces):
        arrived((0, 2), piece)
    halo_step((0, 2))
    project((0, 2), False)
    for piece in low:
        arrived((1, 3), piece)
    project((1, 3), False)
    for piece in high:
        arrived((1, 1), piece)
    halo_step((1, 1))
    project((1, 1), False)
    for piece in range(pieces):
        arrived((1, 2), piece)
    halo_step((1, 2))
    project((1, 2), False)

    hear(2)

    def message(send_buffer, recv_buffer, send_sem, recv_sem, mask):
        other = peer(mask)
        return pltpu.make_async_remote_copy(
            src_ref=send_buffer.at[other],
            dst_ref=recv_buffer.at[ctx],
            send_sem=send_sem.at[mask],
            recv_sem=recv_sem.at[mask],
            device_id={"ctx": other, "tp": tp},
            device_id_type=MESH,
        )

    def p_message(mask):
        return message(psend, precv, p_send, p_recv, mask)

    def y_message(mask):
        return message(ysend, yrecv, y_send, y_recv, mask)

    ident = eye(ROWS, ROWS, 0).astype(BF16)
    per = 128 // PART
    for far, near in ((3, (0, 1, 2, 3)), (2, (2, 3, 0, 1)), (1, (0, 1, 2, 3)), (0, (2, 3, 1))):
        quad = peer(far * per) // per
        lanes = pl.ds(pl.multiple_of(quad * 128, 128), 128)
        branches = []
        for b in range(3):
            ext[b] = total[b, :, lanes].astype(BF16).astype(F32)
            acc = taps_v[b, pl.ds(0, 1), lanes] * ext[b, pl.ds(PAD - TAPS + 1, ROWS)]
            for t in range(1, TAPS):
                acc = acc + taps_v[b, pl.ds(t, 1), lanes] * ext[b, pl.ds(PAD - TAPS + 1 + t, ROWS)]
            branches.append(acc)
        gate[:, lanes] = branches[0]
        product = (branches[1] * branches[2]).astype(BF16)
        turned = nt_dot(ident, product).astype(BF16)
        psend[pl.ds(quad * per, per)] = turned.reshape(per, PART, ROWS)
        for low_mask in near:
            p_message(far * per + low_mask).start()
    precv[pl.ds(ctx, 1)] = psend[pl.ds(ctx, 1)]

    half_blocks = NCTX // 2
    near_masks = [4, 5, 2, 3, 6, 7, 1]
    far_masks = [12, 13, 10, 11, 14, 15, 8, 9]
    skip_row = skip_v[:, pl.ds(pl.multiple_of(ctx // 4 * 128, 128), 128)]
    skip_column = jnp.sum(jnp.where(pick, skip_row, 0.0), axis=1, keepdims=True)

    def blocks_of(half):
        return pl.ds(half * half_blocks, half_blocks)

    def rows_in(half):
        return pl.ds(half * half_blocks * PART, half_blocks * PART)

    def forward(half):
        block_rows = precv[blocks_of(half)].reshape(half_blocks * PART, ROWS)
        spec[rows_in(half)] = dot(block_rows, fh_v[...]) + dot(block_rows, fl_v[...])

    def gather_terms(to_half, from_half, start):
        for block in range(to_half * half_blocks, (to_half + 1) * half_blocks):
            now = pl.ds(block * PART, PART)
            real = jnp.zeros((PART, ROWS), F32) if start else yhat[now, :ROWS]
            imag = jnp.zeros((PART, ROWS), F32) if start else yhat[now, ROWS:]
            for earlier in range(from_half * half_blocks, min(block + 1, (from_half + 1) * half_blocks)):
                lag = pl.ds((block - earlier) * PART, PART)
                src = pl.ds(earlier * PART, PART)
                p_real = spec[src, :ROWS]
                p_imag = spec[src, ROWS:]
                cross = gain_im[lag]
                real = real + gain_re[lag] * p_real - cross * p_imag
                imag = imag + gain_ny[lag] * p_imag + cross * p_real
            yhat[now, :ROWS] = real
            yhat[now, ROWS:] = imag

    def finish(half, masks):
        both = yhat[rows_in(half)]
        upper = both.astype(BF16)
        lower = (both - upper.astype(F32)).astype(BF16)
        convolved = dot(upper, ih_v[...]) + dot(upper, il_v[...]) + dot(lower, ih_v[...])
        direct = skip_column[None] * precv[blocks_of(half)].astype(F32)
        ysend[blocks_of(half)] = (convolved.reshape(half_blocks, PART, ROWS) + direct).astype(BF16)
        for mask in masks:
            y_message(mask).start()

    for mask in near_masks:
        p_message(mask).wait_recv()

    @pl.when(ctx < half_blocks)
    def _():
        forward(0)
        gather_terms(0, 0, True)
        gather_terms(1, 0, True)
        for mask in far_masks:
            p_message(mask).wait_recv()
        forward(1)
        gather_terms(1, 1, False)
        finish(1, far_masks)
        finish(0, near_masks)

    @pl.when(ctx >= half_blocks)
    def _():
        forward(1)
        gather_terms(1, 1, True)
        for mask in far_masks:
            p_message(mask).wait_recv()
        forward(0)
        gather_terms(0, 0, True)
        finish(0, far_masks)
        gather_terms(1, 0, False)
        finish(1, near_masks)

    yrecv[pl.ds(ctx, 1)] = ysend[pl.ds(ctx, 1)]

    def mix(half, masks):
        for mask in masks:
            y_message(mask).wait_recv()
        lanes = pl.ds(pl.multiple_of(half * (CH // 2), CH // 2), CH // 2)
        mixed = nt_dot(ident, yrecv[blocks_of(half)].reshape(CH // 2, ROWS))
        out[:, lanes] = (gate[:, lanes] * mixed).astype(BF16)

    own_half = ctx // half_blocks
    mix(own_half, near_masks)
    mix(1 - own_half, far_masks)

    for mask in near_masks + far_masks:
        p_message(mask).wait_send()
        y_message(mask).wait_send()
    for copy in sent:
        copy.wait_send()

    @pl.when(ctx < NCTX - 1)
    def _():
        halo_copy((0, 0), (0, 0), {"ctx": ctx + 1, "tp": tp}).wait_send()

    @pl.when(ctx > 0)
    def _():
        for src, dst, side in halo_hops:
            halo_copy(src, dst, {"ctx": ctx, "tp": side}).wait_send()


def hand_over(mixed, out):
    out[...] = mixed[...]


def local(tokens, in_weight, conv_weight, filters, skip_gain):
    any_space = pl.BlockSpec(memory_space=pl.ANY)
    dma = pltpu.SemaphoreType.DMA
    pieces = ROWS // SUB
    size = 2 * ROWS
    scratch = [
        pltpu.VMEM((2 * NZ, PAD + ROWS, DEPTH), BF16),
        pltpu.VMEM((3, 2 * NZ * DEPTH, CH), BF16),
        pltpu.VMEM((3, TAPS, CH), F32),
        pltpu.VMEM((NCTX * ROWS, 128), BF16),
        pltpu.VMEM((1, CH), F32),
        pltpu.VMEM((ROWS, size), BF16),
        pltpu.VMEM((ROWS, size), BF16),
        pltpu.VMEM((size, ROWS), BF16),
        pltpu.VMEM((size, ROWS), BF16),
        pltpu.VMEM((3, PAD + ROWS, CH), F32),
        pltpu.VMEM((3, PAD + ROWS, 128), F32),
        pltpu.VMEM((ROWS, CH), F32),
        pltpu.VMEM((NCTX * PART, ROWS), BF16),
        pltpu.VMEM((NCTX * PART, size), F32),
        pltpu.VMEM((NCTX * PART, ROWS), F32),
        pltpu.VMEM((NCTX * PART, ROWS), F32),
        pltpu.VMEM((NCTX * PART, ROWS), F32),
        pltpu.VMEM((NCTX, PART, ROWS), BF16),
        pltpu.VMEM((NCTX, PART, ROWS), BF16),
        pltpu.VMEM((NCTX * PART, size), F32),
        pltpu.VMEM((NCTX, PART, ROWS), BF16),
        pltpu.VMEM((NCTX, PART, ROWS), BF16),
        dma((2 * NZ,)),
        dma((7,)),
        dma((1,)),
        dma((2 * NZ, pieces)),
        dma((2 * NZ, pieces)),
        dma((2 * NZ,)),
        dma((2 * NZ,)),
        dma((NCTX,)),
        dma((NCTX,)),
        dma((NCTX,)),
        dma((NCTX,)),
        pltpu.SemaphoreType.REGULAR((3,)),
    ]
    mixed = pl.pallas_call(
        kernel,
        out_shape=jax.ShapeDtypeStruct((ROWS, CH), BF16),
        in_specs=[any_space] * 9,
        out_specs=pl.BlockSpec(memory_space=pltpu.VMEM),
        scratch_shapes=scratch,
        compiler_params=pltpu.CompilerParams(
            collective_id=0, has_side_effects=True, vmem_limit_bytes=56 * 1024 * 1024
        ),
        name="hyena",
    )(
        tokens,
        jnp.transpose(in_weight, (1, 0, 2)),
        jnp.transpose(conv_weight, (1, 0, 2)),
        filters,
        skip_gain.reshape(1, CH),
        *(jnp.asarray(table) for table in tables()),
    )
    return pl.pallas_call(
        hand_over,
        out_shape=jax.ShapeDtypeStruct((ROWS, CH), BF16),
        in_specs=[pl.BlockSpec(memory_space=pltpu.VMEM)],
        out_specs=pl.BlockSpec(memory_space=pltpu.VMEM),
        name="hand_over",
    )(mixed)


def solution(mesh):
    placed = (P("ctx", "tp"), P(None, None, "tp"), P(None, None, "tp"), P(None, "tp"), P("tp"))
    return jax.shard_map(local, mesh=mesh, in_specs=placed, out_specs=P("ctx", "tp"), check_vma=False)
```

```python
import functools

import jax
import jax.numpy as jnp
import ml_dtypes
import numpy as np
from jax import lax
from jax.experimental import pallas as pl
from jax.experimental.pallas import tpu as pltpu
from jax.sharding import PartitionSpec as P

TAPS = 7
MESH = pl.DeviceIdType.MESH
ROWS = 128
HALO = 8
PAD = 16
DEPTH = 512
CH = 512
NCTX = 16
NZ = 4
PART = CH // NCTX
SUB = 32
F32 = jnp.float32
BF16 = jnp.bfloat16


def split(table):
    high = table.astype(ml_dtypes.bfloat16)
    low = (table - high.astype(np.float64)).astype(ml_dtypes.bfloat16)
    return high, low


def tables():
    size = 2 * ROWS
    time = np.arange(ROWS)[:, None]
    freq = np.arange(ROWS)[None, :]
    angle = 2 * np.pi * (time * freq % size) / size
    imag = -np.sin(angle)
    imag[:, 0] = np.where(np.arange(ROWS) % 2 == 0, 1.0, -1.0)
    forward = np.concatenate([np.cos(angle), imag], 1)
    weight = np.where(np.arange(ROWS) == 0, 1.0, 2.0)[None, :] / size
    back_real = np.cos(angle) * weight
    back_imag = -np.sin(angle) * weight
    back_imag[:, 0] = np.where(np.arange(ROWS) % 2 == 0, 1.0, -1.0) / size
    inverse = np.concatenate([back_real, back_imag], 1).T
    return (*split(forward), *split(inverse))


def nt_dot(left, right):
    return lax.dot_general(left, right, (((1,), (1,)), ((), ())), preferred_element_type=F32)


def dot(left, right):
    return jnp.dot(left, right, preferred_element_type=F32)


def eye(rows, columns, offset):
    row = lax.broadcasted_iota(jnp.int32, (rows, columns), 0)
    column = lax.broadcasted_iota(jnp.int32, (rows, columns), 1)
    return row + offset == column


def kernel(
    tokens, weight, taps, filters, skip, fwd_hi, fwd_lo, inv_hi, inv_lo, out,
    slots, w_v, taps_v, filt_v, skip_v, fh_v, fl_v, ih_v, il_v,
    total, ext, gate, filt_t, spec, gain_re, gain_im, gain_ny, psend, precv, yhat, ysend, yrecv,
    w_sem, load_sem, own_sem, g_send, g_recv, h_send, h_recv, p_send, p_recv, y_send, y_recv, ready,
):
    ctx = lax.axis_index("ctx")
    tp = lax.axis_index("tp")
    y, z = tp // NZ, tp % NZ
    y_side = (1 - y) * NZ + z
    z_up = y * NZ + (z + 1) % NZ
    z_down = y * NZ + (z + NZ - 1) % NZ

    def peer(mask):
        other = ctx
        for bit in (1, 2, 4, 8):
            if mask & bit:
                other = other + bit * (1 - 2 * ((ctx // bit) % 2))
        return other

    for index in range(2 * NZ):
        slots[index, pl.ds(0, PAD)] = jnp.zeros((PAD, DEPTH), BF16)

    barrier = pltpu.get_barrier_semaphore()
    for side in (y_side, z_up, z_down):
        pl.semaphore_signal(barrier, inc=1, device_id={"ctx": ctx, "tp": side}, device_id_type=MESH)
    beside = (ctx + jnp.where(ctx % 2 == 0, NCTX - 1, 1)) % NCTX
    for other in (peer(1), peer(2), peer(4), peer(8), beside):
        pl.semaphore_signal(barrier, inc=1, device_id={"ctx": other, "tp": tp}, device_id_type=MESH)

    def tell(turn):
        pl.semaphore_signal(
            ready.at[turn], inc=1, device_id={"ctx": peer(1 << turn), "tp": tp}, device_id_type=MESH
        )

    def hear(turn):
        pl.semaphore_wait(ready.at[turn], 1)

    loads = [
        pltpu.make_async_copy(src, dst, load_sem.at[index])
        for index, (src, dst) in enumerate(
            [
                (filters.at[:, pl.ds(pl.multiple_of(ctx // 4 * 128, 128), 128)], filt_v),
                (fwd_hi, fh_v),
                (fwd_lo, fl_v),
                (inv_hi, ih_v),
                (inv_lo, il_v),
                (taps, taps_v),
                (skip, skip_v),
            ]
        )
    ]
    own = pltpu.make_async_copy(tokens, slots.at[0, pl.ds(PAD, ROWS)], own_sem.at[0])
    own.start()
    for load in loads:
        load.start()

    def source(dy, dz):
        there = (1 - y) if dy else y
        return there * NZ + (z + dz) % NZ

    def weight_load(dy, dz):
        rows = pl.ds(pl.multiple_of(source(dy, dz) * DEPTH, DEPTH), DEPTH)
        return pltpu.make_async_copy(weight.at[:, rows], w_v.at[:, rows], w_sem.at[dy * NZ + dz])

    order = [(0, 0), (1, 0), (0, 3), (0, 1), (0, 2), (1, 3), (1, 1), (1, 2)]
    for dy, dz in order:
        weight_load(dy, dz).start()

    pl.semaphore_wait(barrier, 8)

    def rows_of(piece):
        return pl.ds(PAD + piece * SUB, SUB)

    pieces = ROWS // SUB
    low = list(range(pieces // 2))
    high = list(range(pieces // 2, pieces))

    def gather_copy(src_slot, piece, dst_slot, side):
        first = src_slot == (0, 0)
        src = tokens.at[pl.ds(piece * SUB, SUB)] if first else slots.at[src_slot[0] * NZ + src_slot[1], rows_of(piece)]
        index = dst_slot[0] * NZ + dst_slot[1]
        return pltpu.make_async_remote_copy(
            src_ref=src,
            dst_ref=slots.at[index, rows_of(piece)],
            send_sem=g_send.at[index, piece],
            recv_sem=g_recv.at[index, piece],
            device_id={"ctx": ctx, "tp": side},
            device_id_type=MESH,
        )

    sent = []

    def send(src_slot, piece, dst_slot, side):
        copy = gather_copy(src_slot, piece, dst_slot, side)
        copy.start()
        sent.append(copy)

    def arrived(slot, piece):
        gather_copy((1, 1), piece, slot, z_up).wait_recv()

    halo_rows = pl.ds(PAD - HALO, HALO)

    def halo_copy(src_slot, dst_slot, device):
        index = dst_slot[0] * NZ + dst_slot[1]
        src = slots.at[src_slot[0] * NZ + src_slot[1], halo_rows]
        if dst_slot == (0, 0):
            src = tokens.at[pl.ds(ROWS - HALO, HALO)]
        return pltpu.make_async_remote_copy(
            src_ref=src,
            dst_ref=slots.at[index, halo_rows],
            send_sem=h_send.at[index],
            recv_sem=h_recv.at[index],
            device_id=device,
            device_id_type=MESH,
        )

    @pl.when(ctx < NCTX - 1)
    def _():
        halo_copy((0, 0), (0, 0), {"ctx": ctx + 1, "tp": tp}).start()

    for a, b in zip(high, low):
        send((0, 0), a, (1, 0), y_side)
        send((0, 0), a, (0, 3), z_up)
        send((0, 0), b, (0, 1), z_down)
        send((0, 0), b, (1, 0), y_side)
    for a, b in zip(high, low):
        send((0, 0), b, (0, 3), z_up)
        send((0, 0), a, (0, 1), z_down)

    halo_hops = [
        ((0, 0), (1, 0), y_side),
        ((0, 0), (0, 3), z_up),
        ((0, 0), (0, 1), z_down),
        ((0, 3), (0, 2), z_up),
        ((1, 0), (1, 3), z_up),
        ((1, 0), (1, 1), z_down),
        ((1, 3), (1, 2), z_up),
    ]

    def halo_arrived(slot):
        halo_copy((0, 1), slot, {"ctx": ctx, "tp": z_up}).wait_recv()

    def halo_from(slot):
        for src, dst, side in halo_hops:
            if src == slot:
                halo_copy(src, dst, {"ctx": ctx, "tp": side}).start()

    def halo_step(slot):
        @pl.when(ctx > 0)
        def _():
            halo_arrived(slot)
            halo_from(slot)

    tell(0)

    for load in loads:
        load.wait()
    pick = eye(PART, 128, ctx % 4 * PART)
    across = nt_dot(pick.astype(BF16), filt_v[...]).astype(BF16)
    for block in range(NCTX):
        filt_t[pl.ds(block * PART, PART)] = across[:, block * ROWS : (block + 1) * ROWS]
    spec[...] = dot(filt_t[...], fh_v[...]) + dot(filt_t[...], fl_v[...])
    lane = lax.broadcasted_iota(jnp.int32, (PART, ROWS), 1)
    swap = jnp.where(lane % 2 == 0, 1.0, -1.0).astype(F32)
    first_lane = lane == 0
    for block in range(NCTX):
        now = pl.ds(block * PART, PART)
        real = spec[now, :ROWS]
        imag = spec[now, ROWS:]
        if block:
            before = pl.ds((block - 1) * PART, PART)
            real = real + swap * spec[before, :ROWS]
            imag = imag + swap * spec[before, ROWS:]
        gain_re[now] = real
        gain_im[now] = jnp.where(first_lane, 0.0, imag)
        gain_ny[now] = jnp.where(first_lane, imag, real)

    own.wait()
    halo_step((0, 0))

    def project(slot, start):
        weight_load(*slot).wait()
        index = slot[0] * NZ + slot[1]
        rows = pl.ds(pl.multiple_of(source(*slot) * DEPTH, DEPTH), DEPTH)

        def branch(b, carry):
            term = dot(slots[index], w_v[b, rows])
            total[b] = term if start else total[b] + term
            return carry

        lax.fori_loop(0, 3, branch, 0)

    hear(0)
    tell(1)
    project((0, 0), True)

    for a, b in zip(high, low):
        arrived((1, 0), a)
        send((1, 0), a, (1, 3), z_up)
        arrived((0, 1), b)
        send((0, 1), b, (0, 2), z_down)
        arrived((0, 3), a)
        send((0, 3), a, (0, 2), z_up)
        arrived((1, 0), b)
        send((1, 0), b, (1, 1), z_down)
    hear(1)
    tell(2)
    halo_step((1, 0))
    project((1, 0), False)
    for a, b in zip(high, low):
        arrived((0, 3), b)
        send((0, 3), b, (1, 3), y_side)
        arrived((0, 1), a)
        send((0, 1), a, (1, 1), y_side)
    halo_step((0, 3))
    halo_step((0, 1))
    project((0, 3), False)
    for a, b in zip(high, low):
        arrived((1, 3), a)
        send((1, 3), a, (1, 2), z_up)
        arrived((1, 1), b)
        send((1, 1), b, (1, 2), z_down)
    halo_step((1, 3))
    project((0, 1), False)
    for piece in range(pieces):
        arrived((0, 2), piece)
    halo_step((0, 2))
    project((0, 2), False)
    for piece in low:
        arrived((1, 3), piece)
    project((1, 3), False)
    for piece in high:
        arrived((1, 1), piece)
    halo_step((1, 1))
    project((1, 1), False)
    for piece in range(pieces):
        arrived((1, 2), piece)
    halo_step((1, 2))
    project((1, 2), False)

    hear(2)

    def message(send_buffer, recv_buffer, send_sem, recv_sem, mask):
        other = peer(mask)
        return pltpu.make_async_remote_copy(
            src_ref=send_buffer.at[other],
            dst_ref=recv_buffer.at[ctx],
            send_sem=send_sem.at[mask],
            recv_sem=recv_sem.at[mask],
            device_id={"ctx": other, "tp": tp},
            device_id_type=MESH,
        )

    def p_message(mask):
        return message(psend, precv, p_send, p_recv, mask)

    def y_message(mask):
        return message(ysend, yrecv, y_send, y_recv, mask)

    ident = eye(ROWS, ROWS, 0).astype(BF16)
    per = 128 // PART
    for far, near in ((3, (0, 1, 2, 3)), (2, (2, 3, 0, 1)), (1, (0, 1, 2, 3)), (0, (2, 3, 1))):
        quad = peer(far * per) // per
        lanes = pl.ds(pl.multiple_of(quad * 128, 128), 128)
        branches = []
        for b in range(3):
            ext[b] = total[b, :, lanes].astype(BF16).astype(F32)
            acc = taps_v[b, pl.ds(0, 1), lanes] * ext[b, pl.ds(PAD - TAPS + 1, ROWS)]
            for t in range(1, TAPS):
                acc = acc + taps_v[b, pl.ds(t, 1), lanes] * ext[b, pl.ds(PAD - TAPS + 1 + t, ROWS)]
            branches.append(acc)
        gate[:, lanes] = branches[0]
        product = (branches[1] * branches[2]).astype(BF16)
        turned = nt_dot(ident, product).astype(BF16)
        psend[pl.ds(quad * per, per)] = turned.reshape(per, PART, ROWS)
        for low_mask in near:
            p_message(far * per + low_mask).start()
    precv[pl.ds(ctx, 1)] = psend[pl.ds(ctx, 1)]

    half_blocks = NCTX // 2
    near_masks = [4, 5, 2, 3, 6, 7, 1]
    far_masks = [12, 13, 10, 11, 14, 15, 8, 9]
    skip_row = skip_v[:, pl.ds(pl.multiple_of(ctx // 4 * 128, 128), 128)]
    skip_column = jnp.sum(jnp.where(pick, skip_row, 0.0), axis=1, keepdims=True)

    def blocks_of(half):
        return pl.ds(half * half_blocks, half_blocks)

    def rows_in(half):
        return pl.ds(half * half_blocks * PART, half_blocks * PART)

    def forward(half):
        block_rows = precv[blocks_of(half)].reshape(half_blocks * PART, ROWS)
        spec[rows_in(half)] = dot(block_rows, fh_v[...]) + dot(block_rows, fl_v[...])

    def gather_terms(to_half, from_half, start):
        for block in range(to_half * half_blocks, (to_half + 1) * half_blocks):
            now = pl.ds(block * PART, PART)
            real = jnp.zeros((PART, ROWS), F32) if start else yhat[now, :ROWS]
            imag = jnp.zeros((PART, ROWS), F32) if start else yhat[now, ROWS:]
            for earlier in range(from_half * half_blocks, min(block + 1, (from_half + 1) * half_blocks)):
                lag = pl.ds((block - earlier) * PART, PART)
                src = pl.ds(earlier * PART, PART)
                p_real = spec[src, :ROWS]
                p_imag = spec[src, ROWS:]
                cross = gain_im[lag]
                real = real + gain_re[lag] * p_real - cross * p_imag
                imag = imag + gain_ny[lag] * p_imag + cross * p_real
            yhat[now, :ROWS] = real
            yhat[now, ROWS:] = imag

    def finish(half, masks):
        both = yhat[rows_in(half)]
        upper = both.astype(BF16)
        lower = (both - upper.astype(F32)).astype(BF16)
        convolved = dot(upper, ih_v[...]) + dot(upper, il_v[...]) + dot(lower, ih_v[...])
        direct = skip_column[None] * precv[blocks_of(half)].astype(F32)
        ysend[blocks_of(half)] = (convolved.reshape(half_blocks, PART, ROWS) + direct).astype(BF16)
        for mask in masks:
            y_message(mask).start()

    for mask in near_masks:
        p_message(mask).wait_recv()

    @pl.when(ctx < half_blocks)
    def _():
        forward(0)
        gather_terms(0, 0, True)
        gather_terms(1, 0, True)
        for mask in far_masks:
            p_message(mask).wait_recv()
        forward(1)
        gather_terms(1, 1, False)
        finish(1, far_masks)
        finish(0, near_masks)

    @pl.when(ctx >= half_blocks)
    def _():
        forward(1)
        gather_terms(1, 1, True)
        for mask in far_masks:
            p_message(mask).wait_recv()
        forward(0)
        gather_terms(0, 0, True)
        finish(0, far_masks)
        gather_terms(1, 0, False)
        finish(1, near_masks)

    yrecv[pl.ds(ctx, 1)] = ysend[pl.ds(ctx, 1)]

    def mix(half, masks):
        for mask in masks:
            y_message(mask).wait_recv()
        lanes = pl.ds(pl.multiple_of(half * (CH // 2), CH // 2), CH // 2)
        mixed = nt_dot(ident, yrecv[blocks_of(half)].reshape(CH // 2, ROWS))
        out[:, lanes] = (gate[:, lanes] * mixed).astype(BF16)

    own_half = ctx // half_blocks
    mix(own_half, near_masks)
    mix(1 - own_half, far_masks)

    for mask in near_masks + far_masks:
        p_message(mask).wait_send()
        y_message(mask).wait_send()
    for copy in sent:
        copy.wait_send()

    @pl.when(ctx < NCTX - 1)
    def _():
        halo_copy((0, 0), (0, 0), {"ctx": ctx + 1, "tp": tp}).wait_send()

    @pl.when(ctx > 0)
    def _():
        for src, dst, side in halo_hops:
            halo_copy(src, dst, {"ctx": ctx, "tp": side}).wait_send()


def local(tokens, in_weight, conv_weight, filters, skip_gain):
    any_space = pl.BlockSpec(memory_space=pl.ANY)
    dma = pltpu.SemaphoreType.DMA
    pieces = ROWS // SUB
    size = 2 * ROWS
    scratch = [
        pltpu.VMEM((2 * NZ, PAD + ROWS, DEPTH), BF16),
        pltpu.VMEM((3, 2 * NZ * DEPTH, CH), BF16),
        pltpu.VMEM((3, TAPS, CH), F32),
        pltpu.VMEM((NCTX * ROWS, 128), BF16),
        pltpu.VMEM((1, CH), F32),
        pltpu.VMEM((ROWS, size), BF16),
        pltpu.VMEM((ROWS, size), BF16),
        pltpu.VMEM((size, ROWS), BF16),
        pltpu.VMEM((size, ROWS), BF16),
        pltpu.VMEM((3, PAD + ROWS, CH), F32),
        pltpu.VMEM((3, PAD + ROWS, 128), F32),
        pltpu.VMEM((ROWS, CH), F32),
        pltpu.VMEM((NCTX * PART, ROWS), BF16),
        pltpu.VMEM((NCTX * PART, size), F32),
        pltpu.VMEM((NCTX * PART, ROWS), F32),
        pltpu.VMEM((NCTX * PART, ROWS), F32),
        pltpu.VMEM((NCTX * PART, ROWS), F32),
        pltpu.VMEM((NCTX, PART, ROWS), BF16),
        pltpu.VMEM((NCTX, PART, ROWS), BF16),
        pltpu.VMEM((NCTX * PART, size), F32),
        pltpu.VMEM((NCTX, PART, ROWS), BF16),
        pltpu.VMEM((NCTX, PART, ROWS), BF16),
        dma((2 * NZ,)),
        dma((7,)),
        dma((1,)),
        dma((2 * NZ, pieces)),
        dma((2 * NZ, pieces)),
        dma((2 * NZ,)),
        dma((2 * NZ,)),
        dma((NCTX,)),
        dma((NCTX,)),
        dma((NCTX,)),
        dma((NCTX,)),
        pltpu.SemaphoreType.REGULAR((3,)),
    ]
    return pl.pallas_call(
        kernel,
        out_shape=pltpu.VMEM((ROWS, CH), BF16),
        in_specs=[any_space] * 9,
        out_specs=pl.BlockSpec(memory_space=pltpu.VMEM),
        scratch_shapes=scratch,
        compiler_params=pltpu.CompilerParams(
            collective_id=0, has_side_effects=True, vmem_limit_bytes=56 * 1024 * 1024
        ),
        name="hyena",
    )(
        tokens,
        jnp.transpose(in_weight, (1, 0, 2)),
        jnp.transpose(conv_weight, (1, 0, 2)),
        filters,
        skip_gain.reshape(1, CH),
        *(jnp.asarray(table) for table in tables()),
    )


def solution(mesh):
    placed = (P("ctx", "tp"), P(None, None, "tp"), P(None, None, "tp"), P(None, "tp"), P("tp"))
    return jax.shard_map(local, mesh=mesh, in_specs=placed, out_specs=P("ctx", "tp"), check_vma=False)
```
